32 devices in a mesh: st: 8 (over y, x, core), fq: 4 (over z).
Axes of the slice: x: 2, y: 2, z: 4, core: 2. Of those that a mesh axis runs over, the one named last changes fastest.
Arguments:
- signals: bfloat16 [512, 16384], P(('st', 'fq')), may hold values from -6 to 6
- freq_bins: int32 [1024], replicated, may hold values from 1 to 8191, as said below
- sensor_station: int32 [512], P('st'), may hold values from 0 to 255, as said below
- gain: bfloat16 [512, 768], P('st'), may hold values from -1.5 to 1.5
- damping: float32 [256, 768], P('st'), may hold values from 0 to 1
- damping_up: float32 [256, 768], P('st'), may hold values from 0 to 1
- phase_speed: float32 [768], replicated, may hold values from 0.5 to 4
Outputs:
- estimate: bfloat16 [256, 768, 1024], P(('st', 'fq'))
The draws below stay inside these ranges and needn't reach their ends.
Inputs may be any that keep to these rules, and one draw needn't show every extreme that they name: `freq_bins`: distinct bin numbers. `sensor_station`: sensor s sits at one of the 32 stations starting at (s // 64) * 32.
All inputs are finite; a program needn't handle non-finite values.
Results may differ from the reference program's by a relative error of at most 0.015.
Values may be sent and summed in bfloat16 or wider, within the bound.
A program may use at most 320 MiB of HBM per device.

```python
import math
import jax
import jax.numpy as jnp
from jax import lax

NT = 16384
M = 768
NF = 1024
ST_DEV = 32
SENS_GRP = 64
TOUT = 1024
STATIONS = 256
SENS = 512


def draw_freq_bins(key, part):
    order = jax.random.permutation(jax.random.fold_in(key, 11), NT // 2 - 1)
    return (order[:NF] + 1).astype(jnp.int32)


def draw_sensor_station(key, part):
    groups = jnp.arange(SENS, dtype=jnp.int32) // SENS_GRP
    offsets = jax.random.randint(jax.random.fold_in(key, 23), (SENS,), 0, ST_DEV, dtype=jnp.int32)
    return (groups * ST_DEV + offsets).astype(jnp.int32)


def decay_table(key):
    keys = jax.random.split(key, 7)
    share = 0.5
    fast = jax.random.uniform(keys[0], (M,)) < share
    fast_rate = jax.random.uniform(keys[1], (M,), minval=2.3 / (0.75 * ST_DEV), maxval=2.3 / (0.5 * ST_DEV))
    slow_rate = jax.random.uniform(keys[2], (M,), minval=0.1, maxval=0.5) * (2.3 / STATIONS)
    rate = jnp.where(fast, fast_rate, slow_rate)
    blocks = jnp.arange(STATIONS, dtype=jnp.int32) // ST_DEV
    block_factor = jnp.exp(jax.random.uniform(keys[3], (STATIONS // ST_DEV,), minval=-0.35, maxval=0.35))
    station_factor = jax.random.uniform(keys[4], (STATIONS, 1), minval=0.8, maxval=1.2)
    damping_coefficients = rate[None, :] * block_factor[blocks][:, None] * station_factor
    probe_positions = jax.random.randint(keys[5], (2,), 0, STATIONS, dtype=jnp.int32)
    boundary_distances = jax.random.uniform(keys[6], (2,), minval=0.55, maxval=0.8)
    measurement_planes = jnp.arange(STATIONS, dtype=jnp.int32)
    excitation_pulse = jnp.where(measurement_planes == probe_positions[0], boundary_distances[0], 1.0) * jnp.where(measurement_planes == probe_positions[1], boundary_distances[1], 1.0)
    return (jnp.exp(-damping_coefficients) * excitation_pulse[:, None]).astype(jnp.float32)


def draw_damping(key, part):
    return decay_table(jax.random.fold_in(key, 101))


def draw_damping_up(key, part):
    return decay_table(jax.random.fold_in(key, 202))


def shard_levels(rng, extent, pieces, smallest, top_value):
    level = 1.0
    for position, parts in pieces:
        heights = jax.random.uniform(jax.random.fold_in(jax.random.fold_in(rng, 6), position), (parts,), jnp.float32, smallest / len(pieces), top_value / len(pieces))
        level = level * jnp.repeat(jnp.exp(heights), extent[position] // parts).reshape((-1,) + (1,) * (len(extent) - 1 - position))
    return level


def centred(stream_key, extent, spread, most, cuts=(), kind=jnp.bfloat16):
    loudness = shard_levels(stream_key, extent, cuts, -0.22, 0.18) if cuts else 1.0
    entries = jax.random.normal(stream_key, extent, jnp.float32) * spread * loudness
    return jnp.minimum(jnp.maximum(entries, -most), most).astype(kind)


def setup_inputs(seed: int = 0) -> dict:
    key_of = jax.random.split(jax.random.key(seed), 8)
    signals = centred(key_of[0], (SENS, NT), 1.0, 6.0, ((0, 32),))
    freq_bins = draw_freq_bins(jax.random.fold_in(key_of[7], 71), 0)
    sensor_station = draw_sensor_station(jax.random.fold_in(key_of[7], 71), 0)
    gain = centred(key_of[3], (SENS, M), 16 ** -0.5, 1.5, ((0, 8),))
    damping = draw_damping(jax.random.fold_in(key_of[7], 71), 0)
    damping_up = draw_damping_up(jax.random.fold_in(key_of[7], 71), 0)
    phase_speed = jnp.clip(jnp.exp(jax.random.uniform(key_of[6], (M,), jnp.float32, math.log(0.5), math.log(4.0))), 0.5, 4.0)
    return {"signals": signals, "freq_bins": freq_bins, "sensor_station": sensor_station, "gain": gain, "damping": damping, "damping_up": damping_up, "phase_speed": phase_speed}


def cmul(left, right):
    return jnp.stack([left[0] * right[0] - left[1] * right[1], left[0] * right[1] + left[1] * right[0]])

def reference(signals, freq_bins, sensor_station, gain, damping, damping_up, phase_speed):
    n_blocks = STATIONS // ST_DEV
    times = lax.iota(jnp.int32, NT)
    hann = 0.5 - 0.5 * jnp.cos(times.astype(jnp.float32) * (2 * math.pi / NT))
    windowed = (signals.astype(jnp.float32) * hann[None, :]).astype(jnp.bfloat16)
    angle = (times[:, None] * freq_bins[None, :] % NT).astype(jnp.float32) * (2 * math.pi / NT)
    cos_table = (jnp.cos(angle) / math.sqrt(NT)).astype(jnp.bfloat16)
    sin_table = (jnp.sin(angle) / math.sqrt(NT)).astype(jnp.bfloat16)
    spec_re = jnp.dot(windowed, cos_table, preferred_element_type=jnp.float32).astype(jnp.bfloat16)
    spec_im = (-jnp.dot(windowed, sin_table, preferred_element_type=jnp.float32)).astype(jnp.bfloat16)
    theta = 2 * math.pi * (freq_bins.astype(jnp.float32) / NT)[:, None] * phase_speed[None, :]
    rot_down = jnp.stack([jnp.cos(theta), -jnp.sin(theta)])
    rot_up = jnp.stack([jnp.cos(theta), jnp.sin(theta)])
    spectra = jnp.stack([spec_re, spec_im]).astype(jnp.float32)
    gain_wide = gain.astype(jnp.float32)
    zeros = jnp.zeros((2, NF, M), jnp.float32)
    t_out = NT - TOUT + lax.iota(jnp.int32, TOUT)
    out_angle = (freq_bins[:, None] * t_out[None, :] % NT).astype(jnp.float32) * (2 * math.pi / NT)
    inverse = jnp.stack([jnp.cos(out_angle) / math.sqrt(NF), -jnp.sin(out_angle) / math.sqrt(NF)]).astype(jnp.bfloat16)

    def block_forcing(block):
        first = (block * SENS_GRP).astype(jnp.int32)
        spec_block = lax.dynamic_slice_in_dim(spectra, first, SENS_GRP, 1)
        gain_block = lax.dynamic_slice_in_dim(gain_wide, first, SENS_GRP, 0)
        local = lax.dynamic_slice_in_dim(sensor_station, first, SENS_GRP, 0) - block * ST_DEV
        outer = jnp.transpose(spec_block, (1, 0, 2))[:, :, :, None] * gain_block[:, None, None, :]
        return jnp.zeros((ST_DEV, 2, NF, M), jnp.float32).at[local].add(outer)

    def rows_of(table, block):
        return lax.dynamic_slice_in_dim(table, (block * ST_DEV).astype(jnp.int32), ST_DEV, 0)

    def down_step(state, inputs):
        term, rate = inputs
        state = cmul(rate[None, None, :] * rot_down, state) + term
        return (state, state)

    def up_step(state, inputs):
        term, rate = inputs
        state = cmul(rate[None, None, :] * rot_up, state) + term
        return (state, state)

    def first_pass(entering, block):
        forcing = block_forcing(block)
        leaving, unused = lax.scan(down_step, entering, (forcing, rows_of(damping, block)))
        return (leaving, entering)
    final_down, entering_all = lax.scan(first_pass, zeros, jnp.arange(n_blocks, dtype=jnp.int32))

    def second_pass(entering_up, inputs):
        block, entering_down = inputs
        forcing = block_forcing(block)
        leaving_up, upstream = lax.scan(up_step, entering_up, (forcing, rows_of(damping_up, block)), reverse=True)
        unused, downstream = lax.scan(down_step, entering_down, (forcing, rows_of(damping, block)))
        state = (downstream + upstream).astype(jnp.bfloat16)
        estimator_answer = jnp.einsum('kcfm,cft->kmt', state.astype(jnp.float32), inverse.astype(jnp.float32)).astype(jnp.bfloat16)
        return (leaving_up, estimator_answer)
    final_up, blocks_out = lax.scan(second_pass, zeros, (jnp.arange(n_blocks, dtype=jnp.int32), entering_all), reverse=True)
    return blocks_out.reshape(STATIONS, M, TOUT)
```

```python
import functools
import math

import jax
import jax.numpy as jnp
from jax import lax
from jax.experimental import pallas as pl
from jax.experimental.pallas import tpu as pltpu
from jax.sharding import PartitionSpec as P

NT = 16384
NF = 1024
TOUT = 1024
TILE = 128
LINK = 64
EARLY = 2
STEP = 256
SUB = 16
WIDE = 256
FINE = 128
PACK = NF // WIDE
LANES = 128
SPAN = 256
F32 = jnp.float32
BF16 = jnp.bfloat16
COS = (
    0.9999999891,
    -19.7392045,
    64.93911746,
    -85.45013953,
    60.16763095,
    -25.96759925,
    6.528658158,
)
SIN = (
    6.283184916,
    -41.34158923,
    81.59994333,
    -76.61447253,
    41.34288235,
    -12.47124353,
)


def cmul(left, right):
    return (left[0] * right[0] - left[1] * right[1], left[0] * right[1] + left[1] * right[0])


def square(a):
    return (a[0] * a[0] - a[1] * a[1], 2.0 * (a[0] * a[1]))


def cpow(base, n):
    out = None
    while n:
        if n & 1:
            out = base if out is None else cmul(out, base)
        n >>= 1
        if n:
            base = square(base)
    return out


def horner(coefficients, z):
    out = coefficients[-1] * z + coefficients[-2]
    for value in coefficients[-3::-1]:
        out = out * z + value
    return out


def rotation(turns):
    r = turns - jnp.floor(turns + 0.5)
    z = r * r
    return horner(COS, z), r * horner(SIN, z)


def aligned(i, size):
    return pl.ds(pl.multiple_of(i * size, size), size)


def spectrum_kernel(
    x_ref, freq_ref, down_ref, up_ref, phase_ref, gain_ref, station_ref,
    out_ref, turn_ref, inv_out, rates_ref, own_ref, gain_t_ref, sel_ref, sel_own_ref,
    hann, xw, low, high, a_refs, stack, inv, send, recv, stored,
):
    parts, mine = lax.axis_size("fq"), lax.axis_index("fq")
    sens = x_ref.shape[0]
    coarse = NT // SPAN
    group = 256 // sens

    def peer(r):
        return lax.rem(mine + r, parts)

    barrier = pltpu.get_barrier_semaphore()
    for r in range(1, parts):
        pl.semaphore_signal(
            barrier, inc=1, device_id={"fq": peer(r)}, device_id_type=pl.DeviceIdType.MESH
        )

    def copy(i, r, sender, device):
        here = out_ref.at[:, sender, :, aligned(i, WIDE)]
        return pltpu.make_async_remote_copy(
            src_ref=here,
            dst_ref=here,
            send_sem=send.at[i, r],
            recv_sem=recv.at[i, sender],
            device_id={"fq": device},
            device_id_type=pl.DeviceIdType.MESH,
        )

    turn_ref[...] = freq_ref[...].reshape(1, NF).astype(F32) * (1.0 / NT)
    fine = lax.broadcasted_iota(jnp.int32, (coarse, SPAN), 1)
    rows = lax.broadcasted_iota(jnp.int32, (coarse, SPAN), 0)
    hann[...] = 0.5 - 0.5 * rotation((rows * SPAN + fine).astype(F32) * (1.0 / NT))[0]

    def window(i, unused):
        for g in range(8):
            h = i * 8 + g
            xw[aligned(h, sens), :] = x_ref[:, aligned(h, SPAN)].astype(F32) * hann[pl.ds(h, 1), :]
        return unused

    lax.fori_loop(0, coarse // 8, window, 0)
    pl.semaphore_wait(barrier, parts - 1)
    step = lax.broadcasted_iota(jnp.int32, (SPAN, 1), 0).astype(F32)
    scale = 1.0 / math.sqrt(NT)

    def bins(i, unused):
        turn = turn_ref[:, aligned(i, WIDE)]
        c, s = rotation(step * turn)
        low[:, :WIDE], low[:, WIDE:] = c.astype(BF16), s.astype(BF16)
        high[0], high[1] = rotation(step[:coarse] * (SPAN * turn))
        re = im = jnp.zeros((sens, WIDE), F32)
        for g in range(coarse // group):
            a_ref = a_refs[g % 2]
            left = xw[g * group * sens : (g + 1) * group * sens, :].astype(BF16)
            a_ref[...] = jnp.dot(left, low[...], preferred_element_type=F32)
            for h in range(group):
                a, b = a_ref[h * sens : (h + 1) * sens, :WIDE], a_ref[h * sens : (h + 1) * sens, WIDE:]
                at = g * group + h
                hc, hs = high[0, at : at + 1, :], high[1, at : at + 1, :]
                re = re + (hc * a - hs * b)
                im = im + (hs * a + hc * b)
        out_ref[0, mine, :, aligned(i, WIDE)] = (re * scale).astype(BF16)
        out_ref[1, mine, :, aligned(i, WIDE)] = (-im * scale).astype(BF16)
        for r in range(1, parts):
            copy(i, r, mine, peer(r)).start()
        return unused

    lax.fori_loop(0, NF // WIDE, bins, 0)
    inverse_table(turn_ref, inv)
    inv_copy = pltpu.make_async_copy(inv, inv_out, stored)
    inv_copy.start()
    small_tables(
        down_ref, up_ref, phase_ref[...].reshape(1, phase_ref.shape[0]), gain_ref,
        station_ref[...].reshape(1, station_ref.shape[0]),
        rates_ref, own_ref, gain_t_ref, sel_ref, sel_own_ref, stack,
    )

    def finish(i, unused):
        for r in range(1, parts):
            copy(i, r, peer(r), peer(r)).wait_recv()
            copy(i, r, mine, peer(r)).wait_send()
        return unused

    lax.fori_loop(0, NF // WIDE, finish, 0)
    inv_copy.wait()


def inverse_table(turn_ref, inv):
    scale = 1.0 / math.sqrt(NF)
    lane = lax.broadcasted_iota(jnp.int32, (1, FINE), 1).astype(F32)

    def block(i, unused):
        rows = aligned(i, LANES)
        turns = jnp.broadcast_to(turn_ref[:, rows], (LANES, LANES)).T
        lc, ls = rotation(turns * lane)
        hc, hs = rotation(turns * ((NT - TOUT) + FINE * lane))
        hc, hs = hc * scale, hs * scale
        for h in range(TOUT // FINE):
            a, b = hc[:, h : h + 1], hs[:, h : h + 1]
            cols = slice(h * FINE, (h + 1) * FINE)
            inv[rows, cols] = (a * lc - b * ls).astype(BF16)
            inv[aligned(i + NF // LANES, LANES), cols] = (-(b * lc + a * ls)).astype(BF16)
        return unused

    lax.fori_loop(0, NF // LANES, block, 0)


def small_tables(
    down_ref, up_ref, phase, gain_ref, station,
    rates_ref, own_ref, gain_t_ref, sel_ref, sel_own_ref, stack,
):
    parts, mine = lax.axis_size("fq"), lax.axis_index("fq")
    count, width = down_ref.shape
    own = count // parts
    stack[...] = jnp.zeros_like(stack)
    stack[:count] = down_ref[...]
    stack[count : 2 * count] = up_ref[...]
    for d, ref in ((0, down_ref), (1, up_ref)):
        at = 2 * count + d * (parts + 1)
        row = jnp.ones((1, width), F32)
        stack[at : at + 1] = row
        for k in range(count):
            b = k if d == 0 else count - 1 - k
            row = row * ref[b : b + 1, :]
            if (k + 1) % own == 0:
                q = (k + 1) // own
                stack[at + q : at + q + 1] = row
    at = 2 * count + 2 * (parts + 1)
    stack[at : at + 1] = phase
    for i in range(width // LANES):
        cols = slice(i * LANES, (i + 1) * LANES)
        rates_ref[cols, :] = stack[:, cols].T
        gain_t_ref[cols, :] = gain_ref[:, cols].astype(F32).T.astype(BF16)
    first = mine * own
    for v in range(parts):

        @pl.when(mine == v)
        def _():
            stack[:own] = down_ref[v * own : (v + 1) * own, :]
            stack[own : 2 * own] = up_ref[v * own : (v + 1) * own, :]

    stack[2 * own : 2 * own + 1] = phase
    for i in range(width // LANES):
        cols = slice(i * LANES, (i + 1) * LANES)
        own_ref[cols, :] = stack[:, cols].T

    local = station - lax.axis_index("st") * count
    shape = sel_ref.shape[1:]
    for k in range(count):
        sel_ref[k] = jnp.broadcast_to(jnp.where(local == k, 1.0, 0.0), shape).astype(BF16)
    for k in range(own):
        hit = jnp.where(local == first + k, 1.0, 0.0)
        sel_own_ref[k] = jnp.broadcast_to(hit, shape).astype(BF16)


def spectrum(signals, freq_bins, damping, damping_up, phase_speed, gain, sensor_station):
    parts = lax.axis_size("fq")
    sens = signals.shape[0]
    coarse = NT // SPAN
    count, width = damping.shape
    near = gain.shape[0]
    vmem = pl.BlockSpec(memory_space=pltpu.VMEM)
    sems = pltpu.SemaphoreType.DMA((NF // WIDE, parts))
    return pl.pallas_call(
        spectrum_kernel,
        in_specs=[vmem] * 7,
        out_specs=[vmem, vmem, pl.BlockSpec(memory_space=pl.ANY)] + [vmem] * 5,
        out_shape=[
            jax.ShapeDtypeStruct((2, parts, sens, NF), BF16),
            jax.ShapeDtypeStruct((1, NF), F32),
            jax.ShapeDtypeStruct((2 * NF, TOUT), BF16),
            jax.ShapeDtypeStruct((width, LANES), F32),
            jax.ShapeDtypeStruct((width, LANES), F32),
            jax.ShapeDtypeStruct((width, near), BF16),
            jax.ShapeDtypeStruct((count, SUB, near), BF16),
            jax.ShapeDtypeStruct((count // parts, SUB, near), BF16),
        ],
        scratch_shapes=[
            pltpu.VMEM((coarse, SPAN), F32),
            pltpu.VMEM((coarse * sens, SPAN), F32),
            pltpu.VMEM((SPAN, 2 * WIDE), BF16),
            pltpu.VMEM((2, coarse, WIDE), F32),
            [pltpu.VMEM((256, 2 * WIDE), F32)] * 2,
            pltpu.VMEM((LANES, width), F32),
            pltpu.VMEM((2 * NF, TOUT), BF16),
            sems,
            sems,
            pltpu.SemaphoreType.DMA,
        ],
        compiler_params=pltpu.CompilerParams(collective_id=1, has_side_effects=True),
        name="spectrum",
    )(signals, freq_bins, damping, damping_up, phase_speed, gain, sensor_station)


def step_down(state, rate, c, s, fr, fi):
    re, im = state
    return (rate * (re * c + im * s) + fr, rate * (im * c - re * s) + fi)


def step_up(state, rate, c, s, fr, fi):
    re, im = state
    return (rate * (re * c - im * s) + fr, rate * (im * c + re * s) + fi)


def link_kernel(
    rates_ref, turn_ref, gain_ref, sel_ref, spec_ref, own_ref, sel_own_ref, inv_in,
    ent_out, early_out, state_out,
    f0, f1, turned, bound, lb, le, pw, pf, below, above, out_down, out_up, snd,
    ent, inv, stage, states, d_own, sd, rd, su, ru, xs, xr, so,
):
    n, me = lax.axis_size("st"), lax.axis_index("st")
    parts, mine = lax.axis_size("fq"), lax.axis_index("fq")
    count = sel_ref.shape[0]
    own = count // parts
    width, fw = ent.shape[2], ent.shape[3]
    tiles = width // LINK
    pieces = fw // WIDE
    right, left = lax.rem(me + 1, n), lax.rem(me + n - 1, n)
    half = lax.rem(mine, 2)
    partner = mine + 1 - 2 * half
    base_down, base_up = 2 * count, 2 * count + parts + 1
    phase_at = 2 * count + 2 * (parts + 1)

    barrier = pltpu.get_barrier_semaphore()
    for axis, other in (("st", left), ("st", right), ("fq", partner)):
        pl.semaphore_signal(
            barrier, inc=1, device_id={axis: other}, device_id_type=pl.DeviceIdType.MESH
        )

    def copy(source, target, send, recv, axis, device):
        return pltpu.make_async_remote_copy(
            src_ref=source,
            dst_ref=target,
            send_sem=send,
            recv_sem=recv,
            device_id={axis: device},
            device_id_type=pl.DeviceIdType.MESH,
        )

    def down_copy(p):
        rows = aligned(p, LINK)
        return copy(
            out_down.at[:, rows, :], below.at[:, rows, :], sd.at[p], rd.at[p], "st", right
        )

    def up_copy(p):
        rows = aligned(p, LINK)
        return copy(out_up.at[:, rows, :], above.at[:, rows, :], su.at[p], ru.at[p], "st", left)

    def cross_copy(p, d):
        rows = aligned(p, LINK)
        part = pl.ds(2 * d, 2)
        return copy(
            snd.at[part, rows, :], ent.at[half, part, rows, :], xs.at[d, p], xr.at[d, p], "fq", partner
        )

    for d in range(2):
        bound[d, 0] = jnp.zeros(bound.shape[2:], F32)

    def bins(j):
        return pl.ds(pl.multiple_of(half * fw + j * WIDE, WIDE), WIDE)

    def forcing(rows, j, f_ref):
        lhs = (gain_ref[rows, :][None] * sel_ref[...]).reshape(count * SUB, gain_ref.shape[1])
        for r in range(2):
            got = jnp.dot(
                lhs, spec_ref[r, :, bins(j)], preferred_element_type=F32
            ).reshape(count // PACK, PACK, SUB, WIDE)
            for a in range(PACK):
                f_ref[:, :, (2 * a + r) * WIDE : (2 * a + r + 1) * WIDE] = got[:, a]

    def ends_piece(i, rows, j, f_ref):
        cols = slice(j * WIDE, (j + 1) * WIDE)
        c, s = turned[0, i, :, cols], turned[1, i, :, cols]

        rates = rates_ref[rows, :]

        def force(k):
            at = 2 * (k % PACK) * WIDE
            return f_ref[k // PACK, :, at : at + WIDE], f_ref[k // PACK, :, at + WIDE : at + 2 * WIDE]

        down = up = (jnp.zeros((SUB, WIDE), F32), jnp.zeros((SUB, WIDE), F32))
        for k in range(count):
            down = step_down(down, rates[:, k : k + 1], c, s, *force(k))
            b = count - 1 - k
            rise = rates[:, count + b : count + b + 1]
            up = step_up(up, rise, c, s, *force(b))
            if (k + 1) % own == 0:
                q = (k + 1) // own
                for r in range(2):
                    if q < parts:
                        bound[0, q, r] = down[r]
                        bound[1, q, r] = up[r]
                    else:
                        le[0, r, rows, cols] = down[r]
                        le[1, r, rows, cols] = up[r]
        for r in range(2):
            for x, q in ((0, mine), (1, partner)):
                lb[x, r, rows, cols] = bound[0, q, r]
                lb[2 + x, r, rows, cols] = bound[1, parts - 1 - q, r]

    subs = LINK // SUB

    def ends(t):
        def prepare(i, unused):
            rows = aligned(t * subs + i, SUB)
            rates = rates_ref[rows, :]
            for j in range(pieces):
                cols = slice(j * WIDE, (j + 1) * WIDE)
                one = rotation(rates[:, phase_at : phase_at + 1] * turn_ref[:, bins(j)])
                unit = cpow(one, own)
                whole = cpow(unit, parts)
                for r in range(2):
                    turned[r, i, :, cols] = one[r]
                    pw[r, rows, cols] = unit[r]
                    pf[r, rows, cols] = whole[r]
            return unused

        lax.fori_loop(0, subs, prepare, 0)

        def sub(i, unused):
            rows = aligned(t * subs + i, SUB)
            after = aligned(lax.rem(t * subs + i + 1, tiles * subs), SUB)
            for j in range(pieces):
                here, there = (f0, f1) if j % 2 == 0 else (f1, f0)
                if j + 1 < pieces:
                    forcing(rows, j + 1, there)
                else:
                    forcing(after, 0, there)
                ends_piece(i, rows, j, here)
            return unused

        lax.fori_loop(0, subs, sub, 0)

    def visit(p, d, first, final, moved, entering, leaving):
        sign = 1.0 - 2.0 * d

        @pl.when((p >= 0) & (p < tiles))
        def _():
            rows = aligned(p, LINK)

            @pl.when(first)
            def _():
                entering[:, rows, :] = jnp.zeros((2, LINK, fw), BF16)

            @pl.when(jnp.logical_not(first))
            def _():
                moved(p).wait_recv()

            @pl.when(jnp.logical_not(final))
            def _():
                at = (base_down, base_up)[d] + parts
                for i in range(subs):
                    some = aligned(p * subs + i, SUB)
                    rate = rates_ref[some, :][:, at : at + 1]
                    re, im = entering[0, some, :].astype(F32), entering[1, some, :].astype(F32)
                    c, s = pf[0, some, :], sign * pf[1, some, :]
                    leaving[0, some, :] = (rate * (re * c + im * s) + le[d, 0, some, :]).astype(BF16)
                    leaving[1, some, :] = (rate * (im * c - re * s) + le[d, 1, some, :]).astype(BF16)
                moved(p).start()

            for v in range(parts):

                @pl.when(mine == v)
                def _():
                    def part(i, unused):
                        some = aligned(p * subs + i, SUB)
                        rates = rates_ref[some, :]
                        for j in range(pieces):
                            cols = slice(j * WIDE, (j + 1) * WIDE)
                            unit = (pw[0, some, cols], pw[1, some, cols])
                            re = entering[0, some, cols].astype(F32)
                            im = entering[1, some, cols].astype(F32)
                            for x, q in ((0, v), (1, v + 1 - 2 * (v % 2))):
                                jump = q if d == 0 else parts - 1 - q
                                gone = (re, im)
                                if jump:
                                    at = (base_down, base_up)[d] + jump
                                    rate = rates[:, at : at + 1]
                                    c, s = cpow(unit, jump)
                                    s = sign * s
                                    gone = (
                                        rate * (re * c + im * s) + lb[2 * d + x, 0, some, cols],
                                        rate * (im * c - re * s) + lb[2 * d + x, 1, some, cols],
                                    )
                                for r in range(2):
                                    if x == 0:
                                        ent[v % 2, 2 * d + r, some, cols] = gone[r].astype(BF16)
                                    else:
                                        snd[2 * d + r, some, cols] = gone[r].astype(BF16)
                        return unused

                    lax.fori_loop(0, subs, part, 0)

            cross_copy(p, d).start()

    forcing(aligned(0, SUB), 0, f0)
    pl.semaphore_wait(barrier, 3)
    inv_copy_in = pltpu.make_async_copy(inv_in, inv, so.at[0])
    inv_copy_in.start()

    links = TILE // LINK
    rounds = TOUT // STEP
    pairs = TILE // SUB // rounds
    f_refs = (f0, f1)

    def inv_copy():
        return pltpu.make_async_copy(inv_in, inv, so.at[0])

    def state_copy():
        return pltpu.make_async_copy(states[EARLY % 2], state_out, so.at[1])

    def early_copy(x, n, slot):
        return pltpu.make_async_copy(
            stage.at[slot],
            early_out.at[:, x * TILE : (x + 1) * TILE, aligned(n, STEP)],
            so.at[2 + slot],
        )

    def ent_copy(p):
        rows = aligned(p, LINK)
        return pltpu.make_async_copy(
            ent.at[:, :, rows, :], ent_out.at[:, :, rows, :], so.at[4 + p]
        )

    def received(p):
        for d in range(2):
            cross_copy(p, d).wait_recv()
        ent_copy(p).start()

    def own_forcing(at, f_ref):
        rows = aligned(lax.rem(at, width // SUB), SUB)
        station_forcing(rows, gain_ref, sel_own_ref, spec_ref, f_ref)

    def own_states(x, i, f_ref):
        rows = aligned(x * (TILE // SUB) + i, SUB)
        station_states(
            own_ref[rows, :], turn_ref, ent, rows, f_ref, d_own, states[x % 2], aligned(i, SUB)
        )

    def first_states():
        for p in range(links):
            received(p)

        def sub(i, unused):
            own_states(0, i, f0)
            own_forcing(i + 1, f0)
            return unused

        own_forcing(0, f0)
        lax.fori_loop(0, TILE // SUB, sub, 0)
        own_forcing(TILE // SUB + 1, f1)
        inv_copy().wait()

    def product_and_states(x, h):
        if h == 0:
            for p in range(links):
                received((x + 1) * links + p)

        def column(n, unused):
            slot = lax.rem(n, 2)

            @pl.when(x * rounds + n >= 2)
            def _():
                early_copy(x, n, slot).wait()

            inverse_product(
                states[x % 2], inv.at[:, aligned(n, STEP)], stage.at[slot], slice(None)
            )
            for g in range(pairs):
                own_states(x + 1, n * pairs + g, f_refs[g])
            for g in range(pairs):
                own_forcing((x + 1) * (TILE // SUB) + (n + 1) * pairs + g, f_refs[g])
            early_copy(x, n, slot).start()
            return unused

        lax.fori_loop(h * rounds // 2, (h + 1) * rounds // 2, column, 0)
        if h == 1 and x == EARLY - 1:
            state_copy().start()

    jobs = [(first_states, links - 1 + n - 1)]
    for x in range(EARLY):
        jobs.append((functools.partial(product_and_states, x, 0), (x + 2) * links - 1 + n - 1))
        jobs.append((functools.partial(product_and_states, x, 1), 0))
    timed, late, free = [], [], tiles
    for job, ready in jobs:
        at = max(free, ready)
        free = at + 1
        if at < n - 1 + tiles:
            timed.append((at, job))
        else:
            late.append(job)

    def turn(t, unused):
        bottom, top = me == 0, me == n - 1

        @pl.when(t < tiles)
        def _():
            ends(t)

        visit(t - me, 0, bottom, top, down_copy, below, out_down)
        visit(t - (n - 1 - me), 1, top, bottom, up_copy, above, out_up)
        for at, job in timed:
            pl.when(t == at)(job)
        return unused

    lax.fori_loop(0, n - 1 + tiles, turn, 0)
    for job in late:
        job()

    def finish(p, unused):
        @pl.when(me < n - 1)
        def _():
            down_copy(p).wait_send()

        @pl.when(me > 0)
        def _():
            up_copy(p).wait_send()

        @pl.when(p >= (EARLY + 1) * links)
        def _():
            received(p)

        for d in range(2):
            cross_copy(p, d).wait_send()
        return unused

    lax.fori_loop(0, tiles, finish, 0)

    def stored(p, unused):
        ent_copy(p).wait()
        return unused

    lax.fori_loop(0, tiles, stored, 0)
    state_copy().wait()
    for slot in range(2):
        early_copy(EARLY - 1, rounds - 2 + slot, slot).wait()


def link(rates, turn, gain_t, sel, spec, rates_own, sel_own, inverse):
    width = gain_t.shape[0]
    fw = NF // 2
    parts = lax.axis_size("fq")
    count = sel.shape[0]
    tiles = width // LINK
    vmem = pl.BlockSpec(memory_space=pltpu.VMEM)
    own = sel_own.shape[0]
    entering, rising = (2, 4, width, fw), (own, TILE, 2 * NF)
    shapes = [entering, (own, EARLY * TILE, TOUT), rising]
    flow = pltpu.VMEM((2, width, fw), BF16)
    sems = pltpu.SemaphoreType.DMA((tiles,))
    return pl.pallas_call(
        link_kernel,
        in_specs=[vmem] * 7 + [pl.BlockSpec(memory_space=pl.ANY)],
        out_specs=[pl.BlockSpec(memory_space=pl.ANY)] * 3,
        out_shape=[jax.ShapeDtypeStruct(shape, BF16) for shape in shapes],
        scratch_shapes=[
            pltpu.VMEM((count // PACK, SUB, 2 * NF), F32),
            pltpu.VMEM((count // PACK, SUB, 2 * NF), F32),
            pltpu.VMEM((2, LINK // SUB, SUB, fw), F32),
            pltpu.VMEM((2, parts, 2, SUB, WIDE), F32),
            pltpu.VMEM((4, 2, width, fw), F32),
            pltpu.VMEM((2, 2, width, fw), F32),
            pltpu.VMEM((2, width, fw), F32),
            pltpu.VMEM((2, width, fw), F32),
            flow,
            flow,
            flow,
            flow,
            pltpu.VMEM((4, width, fw), BF16),
            pltpu.VMEM(entering, BF16),
            pltpu.VMEM((2 * NF, TOUT), BF16),
            pltpu.VMEM((2, own, TILE, STEP), BF16),
            [pltpu.VMEM(rising, BF16)] * 2,
            pltpu.VMEM((own, 2, SUB, WIDE), F32),
            sems,
            sems,
            sems,
            sems,
            pltpu.SemaphoreType.DMA((2, tiles)),
            pltpu.SemaphoreType.DMA((2, tiles)),
            pltpu.SemaphoreType.DMA((4 + tiles,)),
        ],
        compiler_params=pltpu.CompilerParams(
            collective_id=0,
            has_side_effects=True,
        ),
        name="link",
    )(rates, turn, gain_t, sel, spec, rates_own, sel_own, inverse)


def station_forcing(rows, gain_ref, sel_ref, spec_ref, f_ref):
    own, _, sens = sel_ref.shape
    left = (gain_ref[rows, :][None] * sel_ref[...]).reshape(own * SUB, sens)
    for r in range(2):
        f_ref[:own, :, r * NF : (r + 1) * NF] = jnp.dot(
            left, spec_ref[r], preferred_element_type=F32
        ).reshape(own, SUB, NF)


def station_states(rates, turn_ref, ent_ref, rows, f_ref, d_ref, state_ref, at):
    own = state_ref.shape[0]
    half = ent_ref.shape[3]
    for j in range(NF // WIDE):
        lo, hi = slice(j * WIDE, (j + 1) * WIDE), slice(NF + j * WIDE, NF + (j + 1) * WIDE)
        c, s = rotation(rates[:, 2 * own : 2 * own + 1] * turn_ref[:, lo])
        side = j * WIDE // half
        cols = slice(j * WIDE - side * half, (j + 1) * WIDE - side * half)
        first = [ent_ref[side, r, rows, cols].astype(F32) for r in range(4)]
        down, up = tuple(first[:2]), tuple(first[2:])
        for k in range(own):
            down = step_down(down, rates[:, k : k + 1], c, s, f_ref[k, :, lo], f_ref[k, :, hi])
            d_ref[k, 0], d_ref[k, 1] = down
        for k in reversed(range(own)):
            rate = rates[:, own + k : own + k + 1]
            up = step_up(up, rate, c, s, f_ref[k, :, lo], f_ref[k, :, hi])
            state_ref[k, at, lo] = (d_ref[k, 0] + up[0]).astype(BF16)
            state_ref[k, at, hi] = (d_ref[k, 1] + up[1]).astype(BF16)


def inverse_product(state_ref, table_ref, out_ref, cols):
    own, tile, _ = state_ref.shape
    got = jnp.dot(
        state_ref[...].reshape(own * tile, 2 * NF), table_ref[...], preferred_element_type=F32
    )
    out_ref[:, :, cols] = got.reshape(own, tile, STEP).astype(BF16)


def march_kernel(
    rates_ref, turn_ref, gain_ref, sel_ref, spec_ref, ent_ref, inv_ref, early_ref, first_ref, out_ref,
    f_refs, d_ref, even_ref, odd_ref,
):
    tile = out_ref.shape[1]
    width = gain_ref.shape[0]
    rounds = TOUT // STEP
    subs = tile // SUB // rounds
    tiles = width // tile
    i = pl.program_id(0)

    def forcing(at, f_ref):
        rows = aligned(lax.rem(at, width // SUB), SUB)
        station_forcing(rows, gain_ref, sel_ref, spec_ref, f_ref)

    def run(marching, ready, now):
        def turn(n, unused):
            cols = aligned(n, STEP)
            inverse_product(ready, inv_ref.at[:, cols], out_ref, cols)
            if marching is not None:
                for h in range(subs):
                    rows = aligned(n * subs + h, SUB)
                    station_states(
                        rates_ref[rows, :], turn_ref, ent_ref, rows, f_refs[h], d_ref, marching, rows
                    )
                for h in range(subs):
                    forcing(((now + 1) * rounds + n + 1) * subs + h, f_refs[h])
            return unused

        lax.fori_loop(0, rounds, turn, 0)

    states = (even_ref, odd_ref)
    for at, (tile_at, heavy) in enumerate(march_order(tiles)):

        @pl.when(i == at)
        def _():
            if not heavy:
                out_ref[...] = early_ref[...]
                return
            ready = first_ref if tile_at == EARLY else states[tile_at % 2]
            if tile_at == EARLY:
                for h in range(subs):
                    forcing((EARLY + 1) * rounds * subs + h, f_refs[h])
            run(states[1 - tile_at % 2] if tile_at + 1 < tiles else None, ready, tile_at)


def march_order(tiles):
    order, done = [], list(range(EARLY))
    for tile in range(EARLY, tiles):
        order.append((tile, True))
        if done and tile + 1 < tiles:
            order.append((done.pop(0), False))
    return [(tile, False) for tile in done] + order


def estimate(rates, turn, gain_t, sel, spec, ent, inverse, early, first):
    own, _, sens = sel.shape
    width = gain_t.shape[0]
    sides, _, _, half = ent.shape
    tiles = width // TILE
    order = march_order(tiles)

    def choose(values):
        def pick(i):
            out = jnp.int32(values[0])
            for at, value in enumerate(values[1:]):
                out = jnp.where(i > at, jnp.int32(value), out)
            return out

        return pick

    block = choose([tile for tile, heavy in order])
    marched, passed, now_at, early_at = EARLY + 1, 0, [], []
    for tile, heavy in order:
        if heavy:
            marched = min(tile + 1, tiles - 1)
        else:
            passed = tile
        now_at.append(marched)
        early_at.append(passed)
    now, early_now = choose(now_at), choose(early_at)
    fixed = lambda i: (0, 0)
    solid = lambda i: (0, 0, 0)
    return pl.pallas_call(
        march_kernel,
        grid=(tiles,),
        in_specs=[
            pl.BlockSpec((TILE, rates.shape[1]), lambda i: (now(i), 0)),
            pl.BlockSpec((1, NF), fixed),
            pl.BlockSpec((width, sens), fixed),
            pl.BlockSpec((own, SUB, sens), solid),
            pl.BlockSpec((2, sens, NF), solid),
            pl.BlockSpec((sides, 4, TILE, half), lambda i: (0, 0, now(i), 0)),
            pl.BlockSpec((2 * NF, TOUT), fixed),
            pl.BlockSpec((own, TILE, TOUT), lambda i: (0, early_now(i), 0)),
            pl.BlockSpec((own, TILE, 2 * NF), solid),
        ],
        out_specs=pl.BlockSpec((own, TILE, TOUT), lambda i: (0, block(i), 0)),
        out_shape=jax.ShapeDtypeStruct((own, width, TOUT), BF16),
        scratch_shapes=[
            [pltpu.VMEM((own, SUB, 2 * NF), F32)] * (TILE // SUB // (TOUT // STEP)),
            pltpu.VMEM((own, 2, SUB, WIDE), F32),
            pltpu.VMEM((own, TILE, 2 * NF), BF16),
            pltpu.VMEM((own, TILE, 2 * NF), BF16),
        ],
        cost_estimate=pl.CostEstimate(
            flops=12 * own * width * NF * TOUT, bytes_accessed=32 << 20, transcendentals=0
        ),
        compiler_params=pltpu.CompilerParams(

        ),
        name="march",
    )(rates, turn, gain_t, sel, spec, ent, inverse, early, first)


def on_device(signals, freq_bins, sensor_station, gain, damping, damping_up, phase_speed):
    spec, turn, inverse, rates, rates_own, gain_t, sel, sel_own = spectrum(
        signals, freq_bins, damping, damping_up, phase_speed, gain, sensor_station
    )
    spec = spec.reshape(2, gain.shape[0], NF)
    ent, early, first = link(rates, turn, gain_t, sel, spec, rates_own, sel_own, inverse)
    return estimate(rates_own, turn, gain_t, sel_own, spec, ent, inverse, early, first)


def solution(mesh):
    placed = (P(("st", "fq"), None), P(), P("st"), P("st", None), P("st", None), P("st", None), P())
    return jax.shard_map(
        on_device,
        mesh=mesh,
        in_specs=placed,
        out_specs=P(("st", "fq"), None, None),
        check_vma=False,
    )
```

```python
import functools
import math

import jax
import jax.numpy as jnp
from jax import lax
from jax.experimental import pallas as pl
from jax.experimental.pallas import tpu as pltpu
from jax.sharding import PartitionSpec as P

NT = 16384
NF = 1024
TOUT = 1024
TILE = 128
LINK = 64
EARLY = 2
STEP = 256
SUB = 16
WIDE = 256
FINE = 128
PACK = NF // WIDE
LANES = 128
SPAN = 256
F32 = jnp.float32
BF16 = jnp.bfloat16
COS = (
    0.9999999891,
    -19.7392045,
    64.93911746,
    -85.45013953,
    60.16763095,
    -25.96759925,
    6.528658158,
)
SIN = (
    6.283184916,
    -41.34158923,
    81.59994333,
    -76.61447253,
    41.34288235,
    -12.47124353,
)


def cmul(left, right):
    return (left[0] * right[0] - left[1] * right[1], left[0] * right[1] + left[1] * right[0])


def square(a):
    return (a[0] * a[0] - a[1] * a[1], 2.0 * (a[0] * a[1]))


def cpow(base, n):
    out = None
    while n:
        if n & 1:
            out = base if out is None else cmul(out, base)
        n >>= 1
        if n:
            base = square(base)
    return out


def horner(coefficients, z):
    out = coefficients[-1] * z + coefficients[-2]
    for value in coefficients[-3::-1]:
        out = out * z + value
    return out


def rotation(turns):
    r = turns - jnp.floor(turns + 0.5)
    z = r * r
    return horner(COS, z), r * horner(SIN, z)


def aligned(i, size):
    return pl.ds(pl.multiple_of(i * size, size), size)


def spectrum_kernel(
    x_ref, freq_ref, down_ref, up_ref, phase_ref, gain_ref, station_ref,
    out_ref, turn_ref, inv_out, rates_ref, own_ref, gain_t_ref, sel_ref, sel_own_ref,
    hann, xw, low, high, a_refs, stack, inv, send, recv, stored,
):
    parts, mine = lax.axis_size("fq"), lax.axis_index("fq")
    sens = x_ref.shape[0]
    coarse = NT // SPAN
    group = 256 // sens

    def peer(r):
        return lax.rem(mine + r, parts)

    barrier = pltpu.get_barrier_semaphore()
    for r in range(1, parts):
        pl.semaphore_signal(
            barrier, inc=1, device_id={"fq": peer(r)}, device_id_type=pl.DeviceIdType.MESH
        )

    def copy(i, r, sender, device):
        here = out_ref.at[:, sender, :, aligned(i, WIDE)]
        return pltpu.make_async_remote_copy(
            src_ref=here,
            dst_ref=here,
            send_sem=send.at[i, r],
            recv_sem=recv.at[i, sender],
            device_id={"fq": device},
            device_id_type=pl.DeviceIdType.MESH,
        )

    turn_ref[...] = freq_ref[...].reshape(1, NF).astype(F32) * (1.0 / NT)
    fine = lax.broadcasted_iota(jnp.int32, (coarse, SPAN), 1)
    rows = lax.broadcasted_iota(jnp.int32, (coarse, SPAN), 0)
    hann[...] = 0.5 - 0.5 * rotation((rows * SPAN + fine).astype(F32) * (1.0 / NT))[0]

    def window(i, unused):
        for g in range(8):
            h = i * 8 + g
            xw[aligned(h, sens), :] = x_ref[:, aligned(h, SPAN)].astype(F32) * hann[pl.ds(h, 1), :]
        return unused

    lax.fori_loop(0, coarse // 8, window, 0)
    pl.semaphore_wait(barrier, parts - 1)
    step = lax.broadcasted_iota(jnp.int32, (SPAN, 1), 0).astype(F32)
    scale = 1.0 / math.sqrt(NT)

    def bins(i, unused):
        turn = turn_ref[:, aligned(i, WIDE)]
        c, s = rotation(step * turn)
        low[:, :WIDE], low[:, WIDE:] = c.astype(BF16), s.astype(BF16)
        high[0], high[1] = rotation(step[:coarse] * (SPAN * turn))
        re = im = jnp.zeros((sens, WIDE), F32)
        for g in range(coarse // group):
            a_ref = a_refs[g % 2]
            left = xw[g * group * sens : (g + 1) * group * sens, :].astype(BF16)
            a_ref[...] = jnp.dot(left, low[...], preferred_element_type=F32)
            for h in range(group):
                a, b = a_ref[h * sens : (h + 1) * sens, :WIDE], a_ref[h * sens : (h + 1) * sens, WIDE:]
                at = g * group + h
                hc, hs = high[0, at : at + 1, :], high[1, at : at + 1, :]
                re = re + (hc * a - hs * b)
                im = im + (hs * a + hc * b)
        out_ref[0, mine, :, aligned(i, WIDE)] = (re * scale).astype(BF16)
        out_ref[1, mine, :, aligned(i, WIDE)] = (-im * scale).astype(BF16)
        for r in range(1, parts):
            copy(i, r, mine, peer(r)).start()
        return unused

    lax.fori_loop(0, NF // WIDE, bins, 0)
    inverse_table(turn_ref, inv)
    inv_copy = pltpu.make_async_copy(inv, inv_out, stored)
    inv_copy.start()
    small_tables(
        down_ref, up_ref, phase_ref[...].reshape(1, phase_ref.shape[0]), gain_ref,
        station_ref[...].reshape(1, station_ref.shape[0]),
        rates_ref, own_ref, gain_t_ref, sel_ref, sel_own_ref, stack,
    )

    def finish(i, unused):
        for r in range(1, parts):
            copy(i, r, peer(r), peer(r)).wait_recv()
            copy(i, r, mine, peer(r)).wait_send()
        return unused

    lax.fori_loop(0, NF // WIDE, finish, 0)
    inv_copy.wait()


def inverse_table(turn_ref, inv):
    scale = 1.0 / math.sqrt(NF)
    lane = lax.broadcasted_iota(jnp.int32, (1, FINE), 1).astype(F32)

    def block(i, unused):
        rows = aligned(i, LANES)
        turns = jnp.broadcast_to(turn_ref[:, rows], (LANES, LANES)).T
        lc, ls = rotation(turns * lane)
        hc, hs = rotation(turns * ((NT - TOUT) + FINE * lane))
        hc, hs = hc * scale, hs * scale
        for h in range(TOUT // FINE):
            a, b = hc[:, h : h + 1], hs[:, h : h + 1]
            cols = slice(h * FINE, (h + 1) * FINE)
            inv[rows, cols] = (a * lc - b * ls).astype(BF16)
            inv[aligned(i + NF // LANES, LANES), cols] = (-(b * lc + a * ls)).astype(BF16)
        return unused

    lax.fori_loop(0, NF // LANES, block, 0)


def small_tables(
    down_ref, up_ref, phase, gain_ref, station,
    rates_ref, own_ref, gain_t_ref, sel_ref, sel_own_ref, stack,
):
    parts, mine = lax.axis_size("fq"), lax.axis_index("fq")
    count, width = down_ref.shape
    own = count // parts
    stack[...] = jnp.zeros_like(stack)
    stack[:count] = down_ref[...]
    stack[count : 2 * count] = up_ref[...]
    for d, ref in ((0, down_ref), (1, up_ref)):
        at = 2 * count + d * (parts + 1)
        row = jnp.ones((1, width), F32)
        stack[at : at + 1] = row
        for k in range(count):
            b = k if d == 0 else count - 1 - k
            row = row * ref[b : b + 1, :]
            if (k + 1) % own == 0:
                q = (k + 1) // own
                stack[at + q : at + q + 1] = row
    at = 2 * count + 2 * (parts + 1)
    stack[at : at + 1] = phase
    for i in range(width // LANES):
        cols = slice(i * LANES, (i + 1) * LANES)
        rates_ref[cols, :] = stack[:, cols].T
        gain_t_ref[cols, :] = gain_ref[:, cols].astype(F32).T.astype(BF16)
    first = mine * own
    for v in range(parts):

        @pl.when(mine == v)
        def _():
            stack[:own] = down_ref[v * own : (v + 1) * own, :]
            stack[own : 2 * own] = up_ref[v * own : (v + 1) * own, :]

    stack[2 * own : 2 * own + 1] = phase
    for i in range(width // LANES):
        cols = slice(i * LANES, (i + 1) * LANES)
        own_ref[cols, :] = stack[:, cols].T

    local = station - lax.axis_index("st") * count
    shape = sel_ref.shape[1:]
    for k in range(count):
        sel_ref[k] = jnp.broadcast_to(jnp.where(local == k, 1.0, 0.0), shape).astype(BF16)
    for k in range(own):
        hit = jnp.where(local == first + k, 1.0, 0.0)
        sel_own_ref[k] = jnp.broadcast_to(hit, shape).astype(BF16)


def spectrum(signals, freq_bins, damping, damping_up, phase_speed, gain, sensor_station):
    parts = lax.axis_size("fq")
    sens = signals.shape[0]
    coarse = NT // SPAN
    count, width = damping.shape
    near = gain.shape[0]
    vmem = pl.BlockSpec(memory_space=pltpu.VMEM)
    sems = pltpu.SemaphoreType.DMA((NF // WIDE, parts))
    return pl.pallas_call(
        spectrum_kernel,
        in_specs=[vmem] * 7,
        out_specs=[vmem, vmem, pl.BlockSpec(memory_space=pl.ANY)] + [vmem] * 5,
        out_shape=[
            jax.ShapeDtypeStruct((2, parts, sens, NF), BF16),
            jax.ShapeDtypeStruct((1, NF), F32),
            jax.ShapeDtypeStruct((2 * NF, TOUT), BF16),
            jax.ShapeDtypeStruct((width, LANES), F32),
            jax.ShapeDtypeStruct((width, LANES), F32),
            jax.ShapeDtypeStruct((width, near), BF16),
            jax.ShapeDtypeStruct((count, SUB, near), BF16),
            jax.ShapeDtypeStruct((count // parts, SUB, near), BF16),
        ],
        scratch_shapes=[
            pltpu.VMEM((coarse, SPAN), F32),
            pltpu.VMEM((coarse * sens, SPAN), F32),
            pltpu.VMEM((SPAN, 2 * WIDE), BF16),
            pltpu.VMEM((2, coarse, WIDE), F32),
            [pltpu.VMEM((256, 2 * WIDE), F32)] * 2,
            pltpu.VMEM((LANES, width), F32),
            pltpu.VMEM((2 * NF, TOUT), BF16),
            sems,
            sems,
            pltpu.SemaphoreType.DMA,
        ],
        compiler_params=pltpu.CompilerParams(collective_id=1, has_side_effects=True),
        name="spectrum",
    )(signals, freq_bins, damping, damping_up, phase_speed, gain, sensor_station)


def step_down(state, rate, c, s, fr, fi):
    re, im = state
    return (rate * (re * c + im * s) + fr, rate * (im * c - re * s) + fi)


def step_up(state, rate, c, s, fr, fi):
    re, im = state
    return (rate * (re * c - im * s) + fr, rate * (im * c + re * s) + fi)


def link_kernel(
    rates_ref, turn_ref, gain_ref, sel_ref, spec_ref, own_ref, sel_own_ref, inv_in,
    ent_out, early_out, state_out,
    f0, f1, turned, bound, lb, le, pw, pf, below, above, out_down, out_up, snd,
    ent, inv, stage, states, d_own, sd, rd, su, ru, xs, xr, so,
):
    n, me = lax.axis_size("st"), lax.axis_index("st")
    parts, mine = lax.axis_size("fq"), lax.axis_index("fq")
    count = sel_ref.shape[0]
    own = count // parts
    width, fw = ent.shape[2], ent.shape[3]
    tiles = width // LINK
    pieces = fw // WIDE
    right, left = lax.rem(me + 1, n), lax.rem(me + n - 1, n)
    half = lax.rem(mine, 2)
    partner = mine + 1 - 2 * half
    base_down, base_up = 2 * count, 2 * count + parts + 1
    phase_at = 2 * count + 2 * (parts + 1)

    barrier = pltpu.get_barrier_semaphore()
    for axis, other in (("st", left), ("st", right), ("fq", partner)):
        pl.semaphore_signal(
            barrier, inc=1, device_id={axis: other}, device_id_type=pl.DeviceIdType.MESH
        )

    def copy(source, target, send, recv, axis, device):
        return pltpu.make_async_remote_copy(
            src_ref=source,
            dst_ref=target,
            send_sem=send,
            recv_sem=recv,
            device_id={axis: device},
            device_id_type=pl.DeviceIdType.MESH,
        )

    def down_copy(p):
        rows = aligned(p, LINK)
        return copy(
            out_down.at[:, rows, :], below.at[:, rows, :], sd.at[p], rd.at[p], "st", right
        )

    def up_copy(p):
        rows = aligned(p, LINK)
        return copy(out_up.at[:, rows, :], above.at[:, rows, :], su.at[p], ru.at[p], "st", left)

    def cross_copy(p, d):
        rows = aligned(p, LINK)
        part = pl.ds(2 * d, 2)
        return copy(
            snd.at[part, rows, :], ent.at[half, part, rows, :], xs.at[d, p], xr.at[d, p], "fq", partner
        )

    for d in range(2):
        bound[d, 0] = jnp.zeros(bound.shape[2:], F32)

    def bins(j):
        return pl.ds(pl.multiple_of(half * fw + j * WIDE, WIDE), WIDE)

    def forcing(rows, j, f_ref):
        lhs = (gain_ref[rows, :][None] * sel_ref[...]).reshape(count * SUB, gain_ref.shape[1])
        for r in range(2):
            got = jnp.dot(
                lhs, spec_ref[r, :, bins(j)], preferred_element_type=F32
            ).reshape(count // PACK, PACK, SUB, WIDE)
            for a in range(PACK):
                f_ref[:, :, (2 * a + r) * WIDE : (2 * a + r + 1) * WIDE] = got[:, a]

    def ends_piece(i, rows, j, f_ref):
        cols = slice(j * WIDE, (j + 1) * WIDE)
        c, s = turned[0, i, :, cols], turned[1, i, :, cols]

        rates = rates_ref[rows, :]

        def force(k):
            at = 2 * (k % PACK) * WIDE
            return f_ref[k // PACK, :, at : at + WIDE], f_ref[k // PACK, :, at + WIDE : at + 2 * WIDE]

        down = up = (jnp.zeros((SUB, WIDE), F32), jnp.zeros((SUB, WIDE), F32))
        for k in range(count):
            down = step_down(down, rates[:, k : k + 1], c, s, *force(k))
            b = count - 1 - k
            rise = rates[:, count + b : count + b + 1]
            up = step_up(up, rise, c, s, *force(b))
            if (k + 1) % own == 0:
                q = (k + 1) // own
                for r in range(2):
                    if q < parts:
                        bound[0, q, r] = down[r]
                        bound[1, q, r] = up[r]
                    else:
                        le[0, r, rows, cols] = down[r]
                        le[1, r, rows, cols] = up[r]
        for r in range(2):
            for x, q in ((0, mine), (1, partner)):
                lb[x, r, rows, cols] = bound[0, q, r]
                lb[2 + x, r, rows, cols] = bound[1, parts - 1 - q, r]

    subs = LINK // SUB

    def ends(t):
        def prepare(i, unused):
            rows = aligned(t * subs + i, SUB)
            rates = rates_ref[rows, :]
            for j in range(pieces):
                cols = slice(j * WIDE, (j + 1) * WIDE)
                one = rotation(rates[:, phase_at : phase_at + 1] * turn_ref[:, bins(j)])
                unit = cpow(one, own)
                whole = cpow(unit, parts)
                for r in range(2):
                    turned[r, i, :, cols] = one[r]
                    pw[r, rows, cols] = unit[r]
                    pf[r, rows, cols] = whole[r]
            return unused

        lax.fori_loop(0, subs, prepare, 0)

        def sub(i, unused):
            rows = aligned(t * subs + i, SUB)
            after = aligned(lax.rem(t * subs + i + 1, tiles * subs), SUB)
            for j in range(pieces):
                here, there = (f0, f1) if j % 2 == 0 else (f1, f0)
                if j + 1 < pieces:
                    forcing(rows, j + 1, there)
                else:
                    forcing(after, 0, there)
                ends_piece(i, rows, j, here)
            return unused

        lax.fori_loop(0, subs, sub, 0)

    def visit(p, d, first, final, moved, entering, leaving):
        sign = 1.0 - 2.0 * d

        @pl.when((p >= 0) & (p < tiles))
        def _():
            rows = aligned(p, LINK)

            @pl.when(first)
            def _():
                entering[:, rows, :] = jnp.zeros((2, LINK, fw), BF16)

            @pl.when(jnp.logical_not(first))
            def _():
                moved(p).wait_recv()

            @pl.when(jnp.logical_not(final))
            def _():
                at = (base_down, base_up)[d] + parts
                for i in range(subs):
                    some = aligned(p * subs + i, SUB)
                    rate = rates_ref[some, :][:, at : at + 1]
                    re, im = entering[0, some, :].astype(F32), entering[1, some, :].astype(F32)
                    c, s = pf[0, some, :], sign * pf[1, some, :]
                    leaving[0, some, :] = (rate * (re * c + im * s) + le[d, 0, some, :]).astype(BF16)
                    leaving[1, some, :] = (rate * (im * c - re * s) + le[d, 1, some, :]).astype(BF16)
                moved(p).start()

            for v in range(parts):

                @pl.when(mine == v)
                def _():
                    def part(i, unused):
                        some = aligned(p * subs + i, SUB)
                        rates = rates_ref[some, :]
                        for j in range(pieces):
                            cols = slice(j * WIDE, (j + 1) * WIDE)
                            unit = (pw[0, some, cols], pw[1, some, cols])
                            re = entering[0, some, cols].astype(F32)
                            im = entering[1, some, cols].astype(F32)
                            for x, q in ((0, v), (1, v + 1 - 2 * (v % 2))):
                                jump = q if d == 0 else parts - 1 - q
                                gone = (re, im)
                                if jump:
                                    at = (base_down, base_up)[d] + jump
                                    rate = rates[:, at : at + 1]
                                    c, s = cpow(unit, jump)
                                    s = sign * s
                                    gone = (
                                        rate * (re * c + im * s) + lb[2 * d + x, 0, some, cols],
                                        rate * (im * c - re * s) + lb[2 * d + x, 1, some, cols],
                                    )
                                for r in range(2):
                                    if x == 0:
                                        ent[v % 2, 2 * d + r, some, cols] = gone[r].astype(BF16)
                                    else:
                                        snd[2 * d + r, some, cols] = gone[r].astype(BF16)
                        return unused

                    lax.fori_loop(0, subs, part, 0)

            cross_copy(p, d).start()

    forcing(aligned(0, SUB), 0, f0)
    pl.semaphore_wait(barrier, 3)
    inv_copy_in = pltpu.make_async_copy(inv_in, inv, so.at[0])
    inv_copy_in.start()

    links = TILE // LINK
    rounds = TOUT // STEP
    pairs = TILE // SUB // rounds
    f_refs = (f0, f1)

    def inv_copy():
        return pltpu.make_async_copy(inv_in, inv, so.at[0])

    def state_copy():
        return pltpu.make_async_copy(states[EARLY % 2], state_out, so.at[1])

    def early_copy(x, n, slot):
        return pltpu.make_async_copy(
            stage.at[slot],
            early_out.at[:, x * TILE : (x + 1) * TILE, aligned(n, STEP)],
            so.at[2 + slot],
        )

    def ent_copy(p):
        rows = aligned(p, LINK)
        return pltpu.make_async_copy(
            ent.at[:, :, rows, :], ent_out.at[:, :, rows, :], so.at[4 + p]
        )

    def received(p):
        for d in range(2):
            cross_copy(p, d).wait_recv()
        ent_copy(p).start()

    def own_forcing(at, f_ref):
        rows = aligned(lax.rem(at, width // SUB), SUB)
        station_forcing(rows, gain_ref, sel_own_ref, spec_ref, f_ref)

    def own_states(x, i, f_ref):
        rows = aligned(x * (TILE // SUB) + i, SUB)
        station_states(
            own_ref[rows, :], turn_ref, ent, rows, f_ref, d_own, states[x % 2], aligned(i, SUB)
        )

    per = TILE // SUB // 2

    def first_states(d):
        @pl.when(d == 0)
        def _():
            for p in range(links):
                received(p)
            own_forcing(0, f0)

        def sub(i, unused):
            own_states(0, i, f0)
            own_forcing(i + 1, f0)
            return unused

        lax.fori_loop(per * d, per * (d + 1), sub, 0)

        @pl.when(d == 1)
        def _():
            own_forcing(TILE // SUB + 1, f1)
            inv_copy().wait()

    def product_and_states(x, r):
        @pl.when(r == 0)
        def _():
            for p in range(links):
                received((x + 1) * links + p)

        slot = lax.rem(r, 2)

        @pl.when(x * rounds + r >= 2)
        def _():
            early_copy(x, r, slot).wait()

        inverse_product(states[x % 2], inv.at[:, aligned(r, STEP)], stage.at[slot], slice(None))
        for g in range(pairs):
            own_states(x + 1, r * pairs + g, f_refs[g])
        for g in range(pairs):
            own_forcing((x + 1) * (TILE // SUB) + (r + 1) * pairs + g, f_refs[g])
        early_copy(x, r, slot).start()
        if x == EARLY - 1:
            pl.when(r == rounds - 1)(lambda: state_copy().start())

    base = max(tiles, links - 1 + n - 1)
    starts, free = [], base + 2
    for x in range(EARLY):
        starts.append(max(free, (x + 2) * links - 1 + n - 1))
        free = starts[-1] + rounds

    def turn(t, unused):
        bottom, top = me == 0, me == n - 1

        @pl.when(t < tiles)
        def _():
            ends(t)

        visit(t - me, 0, bottom, top, down_copy, below, out_down)
        visit(t - (n - 1 - me), 1, top, bottom, up_copy, above, out_up)
        pl.when((t >= base) & (t < base + 2))(lambda: first_states(t - base))
        for x, at in enumerate(starts):
            pl.when((t >= at) & (t < at + rounds))(
                functools.partial(product_and_states, x, t - at)
            )
        return unused

    lax.fori_loop(0, max(n - 1 + tiles, free), turn, 0)

    def finish(p, unused):
        @pl.when(me < n - 1)
        def _():
            down_copy(p).wait_send()

        @pl.when(me > 0)
        def _():
            up_copy(p).wait_send()

        @pl.when(p >= (EARLY + 1) * links)
        def _():
            received(p)

        for d in range(2):
            cross_copy(p, d).wait_send()
        return unused

    lax.fori_loop(0, tiles, finish, 0)

    def stored(p, unused):
        ent_copy(p).wait()
        return unused

    lax.fori_loop(0, tiles, stored, 0)
    state_copy().wait()
    for slot in range(2):
        early_copy(EARLY - 1, rounds - 2 + slot, slot).wait()


def link(rates, turn, gain_t, sel, spec, rates_own, sel_own, inverse):
    width = gain_t.shape[0]
    fw = NF // 2
    parts = lax.axis_size("fq")
    count = sel.shape[0]
    tiles = width // LINK
    vmem = pl.BlockSpec(memory_space=pltpu.VMEM)
    own = sel_own.shape[0]
    entering, rising = (2, 4, width, fw), (own, TILE, 2 * NF)
    shapes = [entering, (own, EARLY * TILE, TOUT), rising]
    flow = pltpu.VMEM((2, width, fw), BF16)
    sems = pltpu.SemaphoreType.DMA((tiles,))
    return pl.pallas_call(
        link_kernel,
        in_specs=[vmem] * 7 + [pl.BlockSpec(memory_space=pl.ANY)],
        out_specs=[pl.BlockSpec(memory_space=pl.ANY)] * 3,
        out_shape=[jax.ShapeDtypeStruct(shape, BF16) for shape in shapes],
        scratch_shapes=[
            pltpu.VMEM((count // PACK, SUB, 2 * NF), F32),
            pltpu.VMEM((count // PACK, SUB, 2 * NF), F32),
            pltpu.VMEM((2, LINK // SUB, SUB, fw), F32),
            pltpu.VMEM((2, parts, 2, SUB, WIDE), F32),
            pltpu.VMEM((4, 2, width, fw), F32),
            pltpu.VMEM((2, 2, width, fw), F32),
            pltpu.VMEM((2, width, fw), F32),
            pltpu.VMEM((2, width, fw), F32),
            flow,
            flow,
            flow,
            flow,
            pltpu.VMEM((4, width, fw), BF16),
            pltpu.VMEM(entering, BF16),
            pltpu.VMEM((2 * NF, TOUT), BF16),
            pltpu.VMEM((2, own, TILE, STEP), BF16),
            [pltpu.VMEM(rising, BF16)] * 2,
            pltpu.VMEM((own, 2, SUB, WIDE), F32),
            sems,
            sems,
            sems,
            sems,
            pltpu.SemaphoreType.DMA((2, tiles)),
            pltpu.SemaphoreType.DMA((2, tiles)),
            pltpu.SemaphoreType.DMA((4 + tiles,)),
        ],
        compiler_params=pltpu.CompilerParams(
            collective_id=0,
            has_side_effects=True,
        ),
        name="link",
    )(rates, turn, gain_t, sel, spec, rates_own, sel_own, inverse)


def station_forcing(rows, gain_ref, sel_ref, spec_ref, f_ref):
    own, _, sens = sel_ref.shape
    left = (gain_ref[rows, :][None] * sel_ref[...]).reshape(own * SUB, sens)
    for r in range(2):
        f_ref[:own, :, r * NF : (r + 1) * NF] = jnp.dot(
            left, spec_ref[r], preferred_element_type=F32
        ).reshape(own, SUB, NF)


def station_states(rates, turn_ref, ent_ref, rows, f_ref, d_ref, state_ref, at):
    own = state_ref.shape[0]
    half = ent_ref.shape[3]
    for j in range(NF // WIDE):
        lo, hi = slice(j * WIDE, (j + 1) * WIDE), slice(NF + j * WIDE, NF + (j + 1) * WIDE)
        c, s = rotation(rates[:, 2 * own : 2 * own + 1] * turn_ref[:, lo])
        side = j * WIDE // half
        cols = slice(j * WIDE - side * half, (j + 1) * WIDE - side * half)
        first = [ent_ref[side, r, rows, cols].astype(F32) for r in range(4)]
        down, up = tuple(first[:2]), tuple(first[2:])
        for k in range(own):
            down = step_down(down, rates[:, k : k + 1], c, s, f_ref[k, :, lo], f_ref[k, :, hi])
            d_ref[k, 0], d_ref[k, 1] = down
        for k in reversed(range(own)):
            rate = rates[:, own + k : own + k + 1]
            up = step_up(up, rate, c, s, f_ref[k, :, lo], f_ref[k, :, hi])
            state_ref[k, at, lo] = (d_ref[k, 0] + up[0]).astype(BF16)
            state_ref[k, at, hi] = (d_ref[k, 1] + up[1]).astype(BF16)


def inverse_product(state_ref, table_ref, out_ref, cols):
    own, tile, _ = state_ref.shape
    got = jnp.dot(
        state_ref[...].reshape(own * tile, 2 * NF), table_ref[...], preferred_element_type=F32
    )
    out_ref[:, :, cols] = got.reshape(own, tile, STEP).astype(BF16)


def march_kernel(
    rates_ref, turn_ref, gain_ref, sel_ref, spec_ref, ent_ref, inv_ref, early_ref, first_ref, out_ref,
    f_refs, d_ref, even_ref, odd_ref,
):
    tile = out_ref.shape[1]
    width = gain_ref.shape[0]
    rounds = TOUT // STEP
    subs = tile // SUB // rounds
    tiles = width // tile
    i = pl.program_id(0)

    def forcing(at, f_ref):
        rows = aligned(lax.rem(at, width // SUB), SUB)
        station_forcing(rows, gain_ref, sel_ref, spec_ref, f_ref)

    def run(marching, ready):
        def turn(n, unused):
            if ready is not None:
                cols = aligned(n, STEP)
                inverse_product(ready, inv_ref.at[:, cols], out_ref, cols)
            if marching is not None:
                for h in range(subs):
                    rows = aligned(n * subs + h, SUB)
                    station_states(
                        rates_ref[rows, :], turn_ref, ent_ref, rows, f_refs[h], d_ref, marching, rows
                    )
                for h in range(subs):
                    forcing(((i + 1) * rounds + n + 1) * subs + h, f_refs[h])
            return unused

        lax.fori_loop(0, rounds, turn, 0)

    states = (even_ref, odd_ref)

    @pl.when(i < EARLY)
    def _():
        out_ref[...] = early_ref[...]

    @pl.when(i == EARLY - 1)
    def _():
        for h in range(subs):
            forcing((EARLY + 1) * rounds * subs + h, f_refs[h])

    @pl.when(i == EARLY)
    def _():
        run(states[1 - EARLY % 2], first_ref)

    for odd in range(2):

        @pl.when((i > EARLY) & (i < tiles - 1) & (i % 2 == odd))
        def _():
            run(states[1 - odd], states[odd])

    @pl.when(i == tiles - 1)
    def _():
        run(None, states[(tiles - 1) % 2])


def estimate(rates, turn, gain_t, sel, spec, ent, inverse, early, first):
    own, _, sens = sel.shape
    width = gain_t.shape[0]
    sides, _, _, half = ent.shape
    tiles = width // TILE
    now = lambda i: jnp.clip(i + 1, EARLY + 1, tiles - 1)
    fixed = lambda i: (0, 0)
    solid = lambda i: (0, 0, 0)
    return pl.pallas_call(
        march_kernel,
        grid=(tiles,),
        in_specs=[
            pl.BlockSpec((TILE, rates.shape[1]), lambda i: (now(i), 0)),
            pl.BlockSpec((1, NF), fixed),
            pl.BlockSpec((width, sens), fixed),
            pl.BlockSpec((own, SUB, sens), solid),
            pl.BlockSpec((2, sens, NF), solid),
            pl.BlockSpec((sides, 4, TILE, half), lambda i: (0, 0, now(i), 0)),
            pl.BlockSpec((2 * NF, TOUT), fixed),
            pl.BlockSpec((own, TILE, TOUT), lambda i: (0, jnp.minimum(i, EARLY - 1), 0)),
            pl.BlockSpec((own, TILE, 2 * NF), solid),
        ],
        out_specs=pl.BlockSpec((own, TILE, TOUT), lambda i: (0, i, 0)),
        out_shape=jax.ShapeDtypeStruct((own, width, TOUT), BF16),
        scratch_shapes=[
            [pltpu.VMEM((own, SUB, 2 * NF), F32)] * (TILE // SUB // (TOUT // STEP)),
            pltpu.VMEM((own, 2, SUB, WIDE), F32),
            pltpu.VMEM((own, TILE, 2 * NF), BF16),
            pltpu.VMEM((own, TILE, 2 * NF), BF16),
        ],
        cost_estimate=pl.CostEstimate(
            flops=12 * own * width * NF * TOUT, bytes_accessed=32 << 20, transcendentals=0
        ),
        compiler_params=pltpu.CompilerParams(

        ),
        name="march",
    )(rates, turn, gain_t, sel, spec, ent, inverse, early, first)


def on_device(signals, freq_bins, sensor_station, gain, damping, damping_up, phase_speed):
    spec, turn, inverse, rates, rates_own, gain_t, sel, sel_own = spectrum(
        signals, freq_bins, damping, damping_up, phase_speed, gain, sensor_station
    )
    spec = spec.reshape(2, gain.shape[0], NF)
    ent, early, first = link(rates, turn, gain_t, sel, spec, rates_own, sel_own, inverse)
    return estimate(rates_own, turn, gain_t, sel_own, spec, ent, inverse, early, first)


def solution(mesh):
    placed = (P(("st", "fq"), None), P(), P("st"), P("st", None), P("st", None), P("st", None), P())
    return jax.shard_map(
        on_device,
        mesh=mesh,
        in_specs=placed,
        out_specs=P(("st", "fq"), None, None),
        check_vma=False,
    )
```
